32 devices in a mesh: dp: 2 (over core), ep: 16 (over z, y, x).
Axes of the slice: x: 2, y: 2, z: 4, core: 2. Of those that a mesh axis runs over, the one named last changes fastest.
Arguments:
- latent_cache: bfloat16 [16, 4, 512, 576], P('ep', 'dp'), may hold values from -6 to 6
- lengths: int32 [16, 4], P(None, 'dp'), may hold values from 2 to 512
- new_home: int32 [16, 4], P(None, 'dp'), may hold values from 0 to 15, as said below
- queries: bfloat16 [2, 16, 4, 128, 576], P(None, 'ep', 'dp'), may hold values from -32 to 32
- new_latent: bfloat16 [2, 16, 4, 576], P(None, 'ep', 'dp'), may hold values from -6 to 6
- hidden: bfloat16 [2, 16, 4, 3584], P(None, 'ep', 'dp'), may hold values from -6 to 6
- routes: int32 [2, 16, 4, 8], P(None, 'ep', 'dp'), may hold values from 0 to 15, all different within a row; in each aligned block of 4 rows (0 to 3, 4 to 7, ..., all dimensions but the last counted through in order) at most 4 rows name the same one
- route_logits: bfloat16 [2, 16, 4, 8], P(None, 'ep', 'dp'), may hold values from -8 to 8
- w_gate: bfloat16 [16, 3584, 1024], P('ep', None, 'dp'), may hold values from -0.09375 to 0.09375
- w_up: bfloat16 [16, 3584, 1024], P('ep', None, 'dp'), may hold values from -0.09375 to 0.09375
- w_down: bfloat16 [16, 1024, 3584], P('ep', 'dp'), may hold values from -0.1875 to 0.1875
Outputs:
- attended: bfloat16 [2, 16, 4, 128, 512], P(None, 'ep', 'dp')
- moe_out: bfloat16 [2, 16, 4, 3584], P(None, 'ep', 'dp')
The draws below stay inside these ranges and needn't reach their ends.
Inputs may be any that keep to these rules, and one draw needn't show every extreme that they name: `routes`: in each step, the 4 requests of one ep index name any one expert in at most 4 of their choices, and this bound is reached. For each request index c, new_home[., c] exchanges exactly two ep indices and leaves every other one in place, so new_home[new_home[e, c], c] == e; the two indices lie 16 // 2 apart for even c and 1 apart (modulo 16) for odd c.
All inputs are finite; a program needn't handle non-finite values.
Results may differ from the reference program's by a relative error of at most 0.0057.
Values may be sent and summed in bfloat16 or wider, within the bound.
A program may use at most 128 MiB of HBM per device.

```python
import math
import jax
import jax.numpy as jnp
import numpy as np
from jax import lax

D = 3584
FF = 1024
HEADS = 128
KV_RANK = 512
ROPE = 64
HEAD_QK = 192
TOP = 8
STEPS = 2
CACHE = 512
EXPERTS = 16
COLROWS = 4
CAP = 4
N_DP = 2


def integer_parts(key):
    subkeys = jax.random.split(jax.random.fold_in(key, 5), 5)
    heavy_rank = jax.random.randint(subkeys[0], (EXPERTS, 1), 0, 6) == 0
    long_rows = jax.random.randint(subkeys[1], (EXPERTS, COLROWS), CACHE // 2, CACHE + 1)
    short_rows = jax.random.randint(subkeys[2], (EXPERTS, COLROWS), 2, CACHE // 4 + 2)
    flat_lengths = jnp.where(heavy_rank, long_rows, short_rows).reshape(-1)
    total_rows = EXPERTS * COLROWS
    first_spot = jax.random.randint(subkeys[3], (), 0, total_rows)
    second_spot = (first_spot + 1 + jax.random.randint(subkeys[4], (), 0, total_rows - 1)) % total_rows
    spots = jnp.arange(total_rows)
    flat_lengths = jnp.where(spots == first_spot, CACHE, flat_lengths)
    flat_lengths = jnp.where(spots == second_spot, 2, flat_lengths)
    lengths = flat_lengths.reshape(EXPERTS, COLROWS).astype(jnp.int32)
    rank_ids = jnp.arange(EXPERTS, dtype=jnp.int32)[:, None]
    long_score = lengths * EXPERTS + (EXPERTS - 1 - rank_ids)
    heavy_pick = jnp.argmax(long_score, 0).astype(jnp.int32)
    request_ids = jnp.arange(COLROWS, dtype=jnp.int32)
    offset = jnp.where(request_ids % 2 == 0, EXPERTS // 2, 1).astype(jnp.int32)
    light_pick = ((heavy_pick + offset) % EXPERTS).astype(jnp.int32)
    homes = jnp.where(rank_ids == heavy_pick[None, :], light_pick[None, :], jnp.where(rank_ids == light_pick[None, :], heavy_pick[None, :], rank_ids))
    return (lengths, homes.astype(jnp.int32))


def draw_lengths(key, part):
    return integer_parts(key)[0]


def draw_new_home(key, part):
    return integer_parts(key)[1]


def float_parts(key):
    subkeys = jax.random.split(jax.random.fold_in(key, 9), 3)
    lat_width = KV_RANK + ROPE
    cache_shape = (EXPERTS, COLROWS, CACHE, lat_width)
    fresh_shape = (STEPS, EXPERTS, COLROWS, lat_width)
    query_shape = (STEPS, EXPERTS, COLROWS, HEADS, lat_width)
    cache_rows = jax.random.truncated_normal(subkeys[0], -6.0, 6.0, cache_shape, jnp.float32)
    fresh_rows = jax.random.truncated_normal(subkeys[1], -6.0, 6.0, fresh_shape, jnp.float32)
    query_rows = 0.9 * jax.random.truncated_normal(subkeys[2], -6.0, 6.0, query_shape, jnp.float32) + 0.1 * fresh_rows[:, :, :, None, :]
    return (cache_rows.astype(jnp.bfloat16), fresh_rows.astype(jnp.bfloat16), query_rows.astype(jnp.bfloat16))


def draw_latent_cache(key, part):
    return float_parts(key)[0]


def draw_new_latent(key, part):
    return float_parts(key)[1]


def draw_queries(key, part):
    return float_parts(key)[2]


def block_levels(rng, extent, cuts, least, largest):
    gain = 1.0
    for position, parts in cuts:
        heights = jax.random.uniform(jax.random.fold_in(jax.random.fold_in(rng, 6), position), (parts,), jnp.float32, least / len(cuts), largest / len(cuts))
        gain = gain * jnp.repeat(jnp.exp(heights), extent[position] // parts).reshape((-1,) + (1,) * (len(extent) - 1 - position))
    return gain


def assign_block(key, own, number, rows, count, top, most, lean):
    ranking = jax.random.permutation(key, count)
    crowded, ordinary = load_shares(count, rows * top, most, lean, True), load_shares(count, rows * top, most, lean, False)
    places = jnp.arange(count)

    def named(sizes, rotation):
        used = int((sizes > 0).sum())
        fixed = max(1, used // 4)
        shifted = fixed + (places - fixed + rotation * (used - fixed)) % max(1, count - fixed)
        return jnp.zeros((count,), jnp.int32).at[ranking[jnp.where(places < fixed, places, shifted)]].set(jnp.asarray(sizes, jnp.int32))

    sizes = jnp.where(number % 4 == 0, named(crowded, number // 4), named(ordinary, number - number // 4 - 1))
    mixed = jax.random.permutation(jax.random.fold_in(own, 3), count)
    giver, receiver = mixed[0:count // 2 * 2:2], mixed[1:count // 2 * 2:2]
    margin = jnp.minimum(sizes[giver] - 1, most - sizes[receiver]) // 2
    margin = jnp.where((giver == ranking[0]) | (receiver == ranking[0]) | (sizes[receiver] == 0), 0, jnp.maximum(margin, 0))
    shifted = jax.random.randint(jax.random.fold_in(own, 4), (count // 2,), 0, 1 << 20) % (margin + 1)
    sizes = sizes.at[giver].add(-shifted).at[receiver].add(shifted)
    members = jnp.searchsorted(jnp.cumsum(sizes), jnp.arange(rows * top), side="right").astype(jnp.int32)
    listing = members.reshape(top, rows).T
    listing = listing[jax.random.permutation(jax.random.fold_in(own, 1), rows)]
    rotation = jax.random.randint(jax.random.fold_in(own, 2), (rows, 1), 0, top)
    return jnp.take_along_axis(listing, (jnp.arange(top)[None, :] + rotation) % top, axis=1)


def load_shares(amount, total, limit, skew, full):
    portions = [(1 << 20) // math.isqrt(rank ** skew) + 1 for rank in range(1, amount + 1)]
    largest = limit if full else min(limit, max(-(-total // amount), total * portions[0] // sum(portions)))
    least = 1 if total - largest >= amount - 1 else 0
    holding, rest = [largest] + [least] * (amount - 1), total - largest - least * (amount - 1)
    while rest > 0:
        candidates = [i for i in range(1, amount) if holding[i] < largest] or [i for i in range(1, amount) if holding[i] < limit]
        whole, remaining = sum([portions[i] for i in candidates]), rest
        for i in candidates:
            extra = min(limit - holding[i], max(1, remaining * portions[i] // whole), rest)
            holding[i] = holding[i] + extra
            rest = rest - extra
    return np.array(holding)


def gaussian(rng, shape, scale, most, cuts=(), kind=jnp.bfloat16):
    result = scale * jax.random.normal(rng, shape, jnp.float32)
    if cuts:
        result = result * block_levels(rng, shape, cuts, -0.22, 0.18)
    return jnp.clip(result, -most, most).astype(kind)


def setup_inputs(seed: int = 0) -> dict:
    key_of = jax.random.split(jax.random.key(seed), 12)
    latent_cache = draw_latent_cache(jax.random.fold_in(key_of[11], 71), 0)
    lengths = draw_lengths(jax.random.fold_in(key_of[11], 71), 0)
    new_home = draw_new_home(jax.random.fold_in(key_of[11], 71), 0)
    queries = draw_queries(jax.random.fold_in(key_of[11], 71), 0)
    new_latent = draw_new_latent(jax.random.fold_in(key_of[11], 71), 0)
    hidden = gaussian(key_of[5], (STEPS, EXPERTS, COLROWS, D), 1.0, 6.0, ((1, 16), (2, 2)))
    routes_keys = jax.random.split(jax.random.fold_in(key_of[6], 1), STEPS * EXPERTS * COLROWS // COLROWS)
    routes_turns = jax.random.permutation(jax.random.fold_in(key_of[6], 3), STEPS * EXPERTS * COLROWS // COLROWS)
    routes = jax.vmap(lambda own, number: assign_block(jax.random.fold_in(key_of[6], 2), own, number, COLROWS, EXPERTS, TOP, CAP, 2))(routes_keys, routes_turns).reshape((STEPS, EXPERTS, COLROWS, TOP))
    route_logits = gaussian(key_of[7], (STEPS, EXPERTS, COLROWS, TOP), 2.0, 8.0, ((1, 16), (2, 2)))
    w_gate = gaussian(key_of[8], (EXPERTS, D, FF), D ** -0.5, 0.09375, ((0, 16), (2, 2)))
    w_up = gaussian(key_of[9], (EXPERTS, D, FF), D ** -0.5, 0.09375, ((0, 16), (2, 2)))
    w_down = gaussian(key_of[10], (EXPERTS, FF, D), FF ** -0.5, 0.1875, ((0, 16), (1, 2)))
    return dict(latent_cache=latent_cache, lengths=lengths, new_home=new_home, queries=queries, new_latent=new_latent, hidden=hidden, routes=routes, route_logits=route_logits, w_gate=w_gate, w_up=w_up, w_down=w_down)


def attend_one(query_rows, cache_rows, fresh_rows, length):
    step_count, head_count, lat_width = query_rows.shape
    softmax_scale = HEAD_QK ** -0.5
    flat_query = query_rows.reshape(step_count * head_count, lat_width)
    cache_scores = jnp.dot(flat_query, cache_rows.T, preferred_element_type=jnp.float32) * softmax_scale
    key_place = jnp.arange(cache_rows.shape[0], dtype=jnp.int32)
    cache_scores = jnp.where(key_place[None, :] < length, cache_scores, -jnp.inf)
    fresh_scores = jnp.dot(flat_query, fresh_rows.T, preferred_element_type=jnp.float32) * softmax_scale
    row_step = jnp.arange(step_count * head_count, dtype=jnp.int32) // head_count
    fresh_step = jnp.arange(step_count, dtype=jnp.int32)
    fresh_scores = jnp.where(fresh_step[None, :] <= row_step[:, None], fresh_scores, -jnp.inf)
    all_scores = jnp.concatenate([cache_scores, fresh_scores], 1)
    row_max = jnp.max(all_scores, 1, keepdims=True)
    weights = jnp.exp(all_scores - row_max)
    probs_all = (weights / jnp.sum(weights, 1, keepdims=True)).astype(jnp.bfloat16)
    key_values = jnp.concatenate([cache_rows, fresh_rows], 0)[:, :KV_RANK]
    served = jnp.dot(probs_all, key_values, preferred_element_type=jnp.float32).astype(jnp.bfloat16)
    return served.reshape(step_count, head_count, KV_RANK)


def expert(items):
    expert_rows, gate_w, up_w, down_w = items
    gate_part = jnp.dot(expert_rows, gate_w, preferred_element_type=jnp.float32)
    up_part = jnp.dot(expert_rows, up_w, preferred_element_type=jnp.float32)
    hidden_units = lax.optimization_barrier((jax.nn.silu(gate_part) * up_part).astype(jnp.bfloat16))
    slices = hidden_units.astype(jnp.float32).reshape(-1, N_DP, FF // N_DP).transpose(1, 0, 2)
    down_slices = down_w.astype(jnp.float32).reshape(N_DP, FF // N_DP, D)
    slice_out = jnp.einsum("jrf,jfd->jrd", slices, down_slices, precision=lax.Precision.HIGHEST)
    rounded = lax.optimization_barrier(slice_out.astype(jnp.bfloat16))
    return jnp.sum(rounded.astype(jnp.float32), 0)


def reference(latent_cache, lengths, new_home, queries, new_latent, hidden, routes, route_logits, w_gate, w_up, w_down):
    query_cols = jnp.transpose(queries, (1, 2, 0, 3, 4))
    fresh_cols = jnp.transpose(new_latent, (1, 2, 0, 3))

    def per_rank(items):
        cache_rank, length_rank, query_rank, fresh_rank = items
        return jax.vmap(attend_one)(query_rank, cache_rank, fresh_rank, length_rank)

    results = lax.map(per_rank, (latent_cache, lengths, query_cols, fresh_cols))
    relocated = results[new_home, jnp.arange(COLROWS, dtype=jnp.int32)[None, :]]
    attended = jnp.transpose(relocated, (2, 0, 1, 3, 4))

    sigmoid_part = jax.nn.sigmoid(route_logits.astype(jnp.float32))
    gate_weights = 2.5 * sigmoid_part / jnp.sum(sigmoid_part, -1, keepdims=True)
    rank_ids = jnp.arange(EXPERTS, dtype=jnp.int32)
    outputs = []
    for number in range(STEPS):
        flat_routes = routes[number].reshape(EXPERTS, COLROWS * TOP)
        onehot = (flat_routes[:, :, None] == rank_ids[None, None, :]).astype(jnp.int32)
        slot_rank = jnp.sum(jnp.cumsum(onehot, 1) * onehot, 2) - 1
        slot_index = flat_routes * CAP + slot_rank
        tokens = jnp.repeat(hidden[number], TOP, axis=1)
        buffer = jnp.zeros((EXPERTS, EXPERTS * CAP, D), jnp.bfloat16)
        buffer = buffer.at[rank_ids[:, None], slot_index].set(tokens)
        by_expert = buffer.reshape(EXPERTS, EXPERTS, CAP, D).transpose(1, 0, 2, 3).reshape(EXPERTS, EXPERTS * CAP, D)
        expert_out = lax.map(expert, (by_expert, w_gate, w_up, w_down)).reshape(EXPERTS, EXPERTS, CAP, D)
        picked = expert_out[flat_routes, rank_ids[:, None], slot_rank]
        weighted = picked.reshape(EXPERTS, COLROWS, TOP, D) * gate_weights[number][..., None]
        outputs.append(jnp.sum(weighted, 2).astype(jnp.bfloat16))
    moe_out = jnp.stack(outputs, 0)
    return attended, moe_out
```

```python
import jax
import jax.numpy as jnp
from jax import lax
from jax.experimental import pallas as pl
from jax.experimental.pallas import tpu as pltpu
from jax.sharding import PartitionSpec as P

KV_RANK = 512
HEAD_QK = 192


def attend_kernel(length_ref, query_ref, cache_ref, fresh_ref, out_ref):
    step_count, head_count, lat_width = query_ref.shape
    rows = step_count * head_count
    length = length_ref[pl.program_id(0)]
    scale = HEAD_QK ** (-0.5)
    query = query_ref[...].reshape(rows, lat_width)
    keys = cache_ref[...]
    scores = (
        lax.dot_general(
            query, keys, (((1,), (1,)), ((), ())), preferred_element_type=jnp.float32
        )
        * scale
    )
    place = lax.broadcasted_iota(jnp.int32, scores.shape, 1)
    scores = jnp.where(place < length, scores, -jnp.inf)
    row_step = lax.broadcasted_iota(jnp.int32, (rows, 1), 0) // head_count
    wide_query = query.astype(jnp.float32)
    fresh = fresh_ref[...].astype(jnp.float32)
    fresh_scores = []
    row_max = jnp.max(scores, 1, keepdims=True)
    for step in range(step_count):
        one = jnp.sum(wide_query * fresh[step : step + 1], 1, keepdims=True) * scale
        one = jnp.where(row_step >= step, one, -jnp.inf)
        row_max = jnp.maximum(row_max, one)
        fresh_scores.append(one)
    weights = jnp.exp(scores - row_max)
    fresh_weights = [jnp.exp(one - row_max) for one in fresh_scores]
    total = jnp.sum(weights, 1, keepdims=True)
    for one in fresh_weights:
        total = total + one
    probs = (weights / total).astype(jnp.bfloat16)
    served = jnp.dot(probs, keys[:, :KV_RANK], preferred_element_type=jnp.float32)
    for step in range(step_count):
        part = (fresh_weights[step] / total).astype(jnp.bfloat16).astype(jnp.float32)
        served = served + part * fresh[step : step + 1, :KV_RANK]
    out_ref[...] = served.astype(jnp.bfloat16).reshape(step_count, head_count, KV_RANK)


def attend(own_lengths, queries, cache, fresh):
    step_count, _, requests, heads, lat = queries.shape
    keys = cache.shape[2]
    return pl.pallas_call(
        attend_kernel,
        grid_spec=pltpu.PrefetchScalarGridSpec(
            num_scalar_prefetch=1,
            grid=(requests,),
            in_specs=[
                pl.BlockSpec((step_count, None, None, heads, lat), lambda r, n: (0, 0, r, 0, 0)),
                pl.BlockSpec((None, None, keys, lat), lambda r, n: (0, r, 0, 0)),
                pl.BlockSpec((None, step_count, lat), lambda r, n: (r, 0, 0)),
            ],
            out_specs=pl.BlockSpec((None, step_count, heads, KV_RANK), lambda r, n: (r, 0, 0, 0)),
        ),
        out_shape=jax.ShapeDtypeStruct((requests, step_count, heads, KV_RANK), jnp.bfloat16),
        name="attend",
    )(own_lengths, queries, cache, fresh)


def relocate(computed, new_home, ranks, own_rank):
    requests = computed.shape[0]
    half = ranks // 2
    across = [(e, (e + half) % ranks) for e in range(ranks)]
    ahead = [(e, (e + 1) % ranks) for e in range(ranks)]
    behind = [(e, (e - 1) % ranks) for e in range(ranks)]
    even, odd = computed[0::2], computed[1::2]
    far = lax.ppermute(even, "ep", across)
    left = lax.ppermute(odd, "ep", ahead)
    right = lax.ppermute(odd, "ep", behind)
    anchor = new_home[own_rank]
    results = []
    for request in range(requests):
        home, slot = anchor[request], request // 2
        if request % 2 == 0:
            moved = far[slot]
        else:
            moved = jnp.where(home == (own_rank + 1) % ranks, right[slot], left[slot])
        results.append(jnp.where(home == own_rank, computed[request], moved))
    return jnp.stack(results, 1)[:, None]


def shards(
    latent_cache,
    lengths,
    new_home,
    queries,
    new_latent,
    hidden,
    routes,
    route_logits,
    w_gate,
    w_up,
    w_down,
):
    ranks = lax.axis_size("ep")
    own_rank = lax.axis_index("ep")
    step_count, _, requests, width = hidden.shape
    own_rows = step_count * requests
    slices = lax.axis_size("dp")

    def shift(value, step):
        return lax.ppermute(value, "dp", [(i, (i + step) % slices) for i in range(slices)])

    rows = hidden.reshape(own_rows, width)
    copies = jnp.broadcast_to(rows[None], (ranks, own_rows, width))
    mine = lax.all_to_all(copies, "ep", split_axis=0, concat_axis=0, tiled=True)
    mine = mine.reshape(ranks * own_rows, width)

    computed = attend(
        lengths[own_rank], queries, latent_cache, jnp.swapaxes(new_latent[:, 0], 0, 1)
    )
    attended = relocate(computed, new_home, ranks, own_rank)

    tokens = jnp.concatenate([mine] + [shift(mine, step) for step in range(1, slices)], 0)
    gate_part = jnp.dot(tokens, w_gate[0], preferred_element_type=jnp.float32)
    up_part = jnp.dot(tokens, w_up[0], preferred_element_type=jnp.float32)
    units = (jax.nn.silu(gate_part) * up_part).astype(jnp.bfloat16)
    slice_out = jnp.dot(units, w_down[0], preferred_element_type=jnp.float32).astype(jnp.bfloat16)
    parts = slice_out.reshape(slices, ranks * own_rows, width)
    whole = parts[0].astype(jnp.float32)
    for step in range(1, slices):
        whole = whole + shift(parts[step], -step).astype(jnp.float32)
    whole = whole.astype(jnp.bfloat16)
    returned = lax.all_to_all(
        whole.reshape(ranks, own_rows, width), "ep", split_axis=0, concat_axis=0, tiled=True
    )

    sigmoid_part = jax.nn.sigmoid(route_logits[:, 0].astype(jnp.float32))
    gates = 2.5 * sigmoid_part / jnp.sum(sigmoid_part, -1, keepdims=True)
    rank_ids = jnp.arange(ranks, dtype=jnp.int32)
    chosen = routes[:, 0, :, :, None] == rank_ids
    dense = jnp.sum(jnp.where(chosen, gates[..., None], 0.0), 2).reshape(own_rows, ranks)
    summed = jnp.sum(returned.astype(jnp.float32) * dense.T[:, :, None], 0)
    moe_out = summed.astype(jnp.bfloat16).reshape(step_count, 1, requests, width)
    return (attended, moe_out)


def solution(mesh):
    placed = (
        P("ep", "dp", None, None),
        P(None, "dp"),
        P(None, "dp"),
        P(None, "ep", "dp", None, None),
        P(None, "ep", "dp", None),
        P(None, "ep", "dp", None),
        P(None, "ep", "dp", None),
        P(None, "ep", "dp", None),
        P("ep", None, "dp"),
        P("ep", None, "dp"),
        P("ep", "dp", None),
    )
    return jax.shard_map(
        shards,
        mesh=mesh,
        in_specs=placed,
        out_specs=(P(None, "ep", "dp", None, None), P(None, "ep", "dp", None)),
        check_vma=False,
    )
```

```python
import jax
import jax.numpy as jnp
from jax import lax
from jax.experimental import pallas as pl
from jax.experimental.pallas import tpu as pltpu
from jax.sharding import PartitionSpec as P


KV_RANK = 512
HEAD_QK = 192


def attend_kernel(length_ref, query_ref, cache_ref, fresh_ref, out_ref):
    step_count, head_count, lat_width = query_ref.shape
    rows = step_count * head_count
    length = length_ref[pl.program_id(0)]
    scale = HEAD_QK ** (-0.5)
    query = query_ref[...].reshape(rows, lat_width)
    keys = cache_ref[...]
    scores = (
        lax.dot_general(
            query, keys, (((1,), (1,)), ((), ())), preferred_element_type=jnp.float32
        )
        * scale
    )
    place = lax.broadcasted_iota(jnp.int32, scores.shape, 1)
    scores = jnp.where(place < length, scores, -jnp.inf)
    row_step = lax.broadcasted_iota(jnp.int32, (rows, 1), 0) // head_count
    wide_query = query.astype(jnp.float32)
    fresh = fresh_ref[...].astype(jnp.float32)
    fresh_scores = []
    row_max = jnp.max(scores, 1, keepdims=True)
    for step in range(step_count):
        one = jnp.sum(wide_query * fresh[step : step + 1], 1, keepdims=True) * scale
        one = jnp.where(row_step >= step, one, -jnp.inf)
        row_max = jnp.maximum(row_max, one)
        fresh_scores.append(one)
    weights = jnp.exp(scores - row_max)
    fresh_weights = [jnp.exp(one - row_max) for one in fresh_scores]
    total = jnp.sum(weights, 1, keepdims=True)
    for one in fresh_weights:
        total = total + one
    probs = (weights / total).astype(jnp.bfloat16)
    served = jnp.dot(probs, keys[:, :KV_RANK], preferred_element_type=jnp.float32)
    for step in range(step_count):
        part = (fresh_weights[step] / total).astype(jnp.bfloat16).astype(jnp.float32)
        served = served + part * fresh[step : step + 1, :KV_RANK]
    out_ref[...] = served.astype(jnp.bfloat16).reshape(step_count, head_count, KV_RANK)


def attend(own_lengths, queries, cache, fresh):
    step_count, _, requests, heads, lat = queries.shape
    keys = cache.shape[2]
    return pl.pallas_call(
        attend_kernel,
        grid_spec=pltpu.PrefetchScalarGridSpec(
            num_scalar_prefetch=1,
            grid=(requests,),
            in_specs=[
                pl.BlockSpec((step_count, None, None, heads, lat), lambda r, n: (0, 0, r, 0, 0)),
                pl.BlockSpec((None, None, keys, lat), lambda r, n: (0, r, 0, 0)),
                pl.BlockSpec((None, step_count, lat), lambda r, n: (r, 0, 0)),
            ],
            out_specs=pl.BlockSpec((None, step_count, heads, KV_RANK), lambda r, n: (r, 0, 0, 0)),
        ),
        out_shape=jax.ShapeDtypeStruct((requests, step_count, heads, KV_RANK), jnp.bfloat16),
        name="attend",
    )(own_lengths, queries, cache, fresh)


def travel(even, odd, ranks):
    half = ranks // 2
    across = [(e, (e + half) % ranks) for e in range(ranks)]
    ahead = [(e, (e + 1) % ranks) for e in range(ranks)]
    behind = [(e, (e - 1) % ranks) for e in range(ranks)]
    far = lax.ppermute(even, "ep", across)
    left = lax.ppermute(odd, "ep", ahead)
    right = lax.ppermute(odd, "ep", behind)
    return far, left, right


def relocate(computed, arrived, new_home, ranks, own_rank):
    requests = computed.shape[0]
    far, left, right = arrived
    anchor = new_home[own_rank]
    results = []
    for request in range(requests):
        home, slot = anchor[request], request // 2
        if request % 2 == 0:
            moved = far[slot]
        else:
            moved = jnp.where(home == (own_rank + 1) % ranks, right[slot], left[slot])
        results.append(jnp.where(home == own_rank, computed[request], moved))
    return jnp.stack(results, 1)[:, None]


def shards(
    latent_cache,
    lengths,
    new_home,
    queries,
    new_latent,
    hidden,
    routes,
    route_logits,
    w_gate,
    w_up,
    w_down,
):
    ranks = lax.axis_size("ep")
    own_rank = lax.axis_index("ep")
    step_count, _, requests, width = hidden.shape
    own_rows = step_count * requests
    slices = lax.axis_size("dp")

    def shift(value, step):
        return lax.ppermute(value, "dp", [(i, (i + step) % slices) for i in range(slices)])

    rows = hidden.reshape(own_rows, width)
    copies = jnp.broadcast_to(rows[None], (ranks, own_rows, width))
    mine = lax.all_to_all(copies, "ep", split_axis=0, concat_axis=0, tiled=True)
    mine = mine.reshape(ranks * own_rows, width)

    computed = attend(
        lengths[own_rank], queries, latent_cache, jnp.swapaxes(new_latent[:, 0], 0, 1)
    )
    mine, computed, even, odd = lax.optimization_barrier(
        (mine, computed, computed[0::2], computed[1::2])
    )
    arrived = travel(even, odd, ranks)

    tokens = jnp.concatenate([mine] + [shift(mine, step) for step in range(1, slices)], 0)
    gate_part = jnp.dot(tokens, w_gate[0], preferred_element_type=jnp.float32)
    up_part = jnp.dot(tokens, w_up[0], preferred_element_type=jnp.float32)
    units = (jax.nn.silu(gate_part) * up_part).astype(jnp.bfloat16)
    slice_out = jnp.dot(units, w_down[0], preferred_element_type=jnp.float32)
    slice_out = slice_out.astype(jnp.bfloat16)
    parts = slice_out.reshape(slices, ranks * own_rows, width)
    whole = parts[0].astype(jnp.float32)
    for step in range(1, slices):
        whole = whole + shift(parts[step], -step).astype(jnp.float32)
    whole = whole.astype(jnp.bfloat16)
    whole, arrived = lax.optimization_barrier((whole, arrived))
    returned = lax.all_to_all(
        whole.reshape(ranks, own_rows, width), "ep", split_axis=0, concat_axis=0, tiled=True
    )

    attended = relocate(computed, arrived, new_home, ranks, own_rank)
    sigmoid_part = jax.nn.sigmoid(route_logits[:, 0].astype(jnp.float32))
    gates = 2.5 * sigmoid_part / jnp.sum(sigmoid_part, -1, keepdims=True)
    rank_ids = jnp.arange(ranks, dtype=jnp.int32)
    chosen = routes[:, 0, :, :, None] == rank_ids
    dense = jnp.sum(jnp.where(chosen, gates[..., None], 0.0), 2).reshape(own_rows, ranks)
    summed = jnp.sum(returned.astype(jnp.float32) * dense.T[:, :, None], 0)
    moe_out = summed.astype(jnp.bfloat16).reshape(step_count, 1, requests, width)
    return (attended, moe_out)


def solution(mesh):
    placed = (
        P("ep", "dp", None, None),
        P(None, "dp"),
        P(None, "dp"),
        P(None, "ep", "dp", None, None),
        P(None, "ep", "dp", None),
        P(None, "ep", "dp", None),
        P(None, "ep", "dp", None),
        P(None, "ep", "dp", None),
        P("ep", None, "dp"),
        P("ep", None, "dp"),
        P("ep", "dp", None),
    )
    return jax.shard_map(
        shards,
        mesh=mesh,
        in_specs=placed,
        out_specs=(P(None, "ep", "dp", None, None), P(None, "ep", "dp", None)),
        check_vma=False,
    )
```
